32 devices in a mesh: blk: 8 (over y, x, core), rows: 4 (over z).
Axes of the slice: x: 2, y: 2, z: 4, core: 2. Of those that a mesh axis runs over, the one named last changes fastest.
Arguments:
- covariance: float32 [16384, 8, 8, 256], P('rows', None, 'blk'), may hold values from 0 to 5, as said below
- panel_order: int32 [64], replicated, may hold values from 0 to 63, each once
Outputs:
- factored: float32 [16384, 8, 8, 256], P('rows', None, 'blk')
The draws below stay inside these ranges and needn't reach their ends.
Inputs may be any that keep to these rules, and one draw needn't show every extreme that they name: covariance is symmetric and positive definite. `panel_order`: every panel appears once; panel j is held by index j % 8 of blk.
All inputs are finite; a program needn't handle non-finite values.
Results may differ from the reference program's by a relative error of at most 0.0003.
Values sent between devices are 32-bit elements; how exact they have to be, the bound alone decides.
A program may use at most 192 MiB of HBM per device.

```python
import jax
import jax.numpy as jnp
from jax import lax

ORDER = 16384
PANEL = 256
SECTIONS = 2
PANELS = 64
OWNERS = 8
PAN_DEV = 8


def draw_covariance(key, part):
    base_key = jax.random.fold_in(key, 11)
    point_key = jax.random.fold_in(base_key, 0)
    points = jax.random.uniform(point_key, (ORDER, 3), jnp.float32)
    squared = jnp.zeros((ORDER, ORDER), jnp.float32)
    for axis_index in range(3):
        column = points[:, axis_index]
        spread_gap = column[:, None] - column[None, :]
        squared = squared + spread_gap * spread_gap
    distance = jnp.sqrt(squared)
    kernel = jnp.exp(-distance / 0.2)
    indices = jnp.arange(ORDER)
    kernel = jnp.where(indices[:, None] == indices[None, :], kernel + 0.25, kernel)
    return kernel.reshape(ORDER, PAN_DEV, OWNERS, PANEL)


def setup_inputs(seed: int = 0) -> dict:
    seeds = jax.random.split(jax.random.key(seed), 3)
    covariance = draw_covariance(jax.random.fold_in(seeds[2], 71), 0)
    panel_order = jax.random.permutation(seeds[1], PANELS).astype(jnp.int32)
    return dict(covariance=covariance, panel_order=panel_order)


def inverse_factor(diagonal_block):
    lower_factor = jnp.linalg.cholesky(diagonal_block)
    identity_block = jnp.eye(diagonal_block.shape[0], dtype=diagonal_block.dtype)
    return lax.linalg.triangular_solve(lower_factor, identity_block, left_side=True, lower=True)

def reference(covariance, panel_order):
    matrix_order = covariance.shape[0]
    panel_width = covariance.shape[3]
    panel_total = matrix_order // panel_width
    working = covariance.reshape(matrix_order, matrix_order)
    frozen = jnp.zeros((panel_total,), jnp.float32)
    for round_index in range(SECTIONS):
        target = panel_order[round_index]
        first_column = (target * panel_width).astype(jnp.int32)
        column_panel = lax.dynamic_slice_in_dim(working, first_column, panel_width, 1)
        diagonal_block = lax.dynamic_slice_in_dim(column_panel, first_column, panel_width, 0)
        inverse = inverse_factor(diagonal_block)
        factor = jnp.dot(column_panel.astype(jnp.float32), inverse.T.astype(jnp.float32), precision=lax.Precision.HIGHEST, preferred_element_type=jnp.float32)
        frozen = frozen + (jnp.arange(panel_total) == target).astype(jnp.float32)
        live_rows = jnp.repeat(1.0 - frozen, panel_width)
        masked_factor = factor * live_rows[:, None]
        working = working - jnp.dot(factor.astype(jnp.float32), masked_factor.T.astype(jnp.float32), precision=lax.Precision.HIGHEST, preferred_element_type=jnp.float32)
        working = lax.dynamic_update_slice_in_dim(working, factor, first_column, 1)
    return working.reshape(covariance.shape)
```

```python
import functools

import jax
import jax.numpy as jnp
from jax import lax
from jax.experimental import pallas as pl
from jax.experimental.pallas import tpu as pltpu
from jax.sharding import PartitionSpec as P

SECTIONS = 2
LANES = 128
HOP = 2
TILE = 128
ROWS = 512
MESH = pl.DeviceIdType.MESH
HIGHEST = lax.Precision.HIGHEST


def split(values):
    high = values.astype(jnp.bfloat16)
    low = (values - high.astype(jnp.float32)).astype(jnp.bfloat16)
    return high, low


CHUNKS = 16


def gather_kernel(order_ref, covariance_ref, panels_ref, blocks_ref, sems):
    me = lax.axis_index("blk")
    z = lax.axis_index("rows")
    owners = lax.axis_size("blk")
    row_count, _, _, width = covariance_ref.shape
    row_panels = row_count // width
    targets = [order_ref[section] for section in range(SECTIONS)]
    mine = [lax.rem(target, owners) == me for target in targets]

    def fetch(section, i):
        rows = pl.ds(i * width, width)
        return pltpu.make_async_copy(
            covariance_ref.at[rows, lax.div(targets[section], owners), 0, :],
            panels_ref.at[rows, pl.ds(section * width, width)],
            sems.at[section, i],
        )

    for section in range(SECTIONS):
        @pl.when(mine[section])
        def _():
            for i in range(row_panels):
                fetch(section, i).start()

        @pl.when(jnp.logical_not(mine[section]))
        def _():
            panels_ref[:, section * width : (section + 1) * width] = jnp.zeros((row_count, width), jnp.float32)

    for section in range(SECTIONS):
        @pl.when(mine[section])
        def _():
            for i in range(row_panels):
                fetch(section, i).wait()

    at = 0
    for r in range(SECTIONS):
        for c in range(r + 1):
            root = lax.div(targets[r], row_panels)
            rows = pl.ds(pl.multiple_of(lax.rem(targets[r], row_panels) * width, width), width)
            seen = panels_ref[rows, c * width : (c + 1) * width]
            blocks_ref[at : at + width, :] = jnp.where(root == z, seen, 0.0)
            at += width


def gather(order, covariance):
    row_count, _, _, width = covariance.shape
    count = SECTIONS * (SECTIONS + 1) // 2
    memory = pl.BlockSpec(memory_space=pltpu.VMEM)
    return pl.pallas_call(
        gather_kernel,
        out_shape=(
            jax.ShapeDtypeStruct((row_count, SECTIONS * width), jnp.float32),
            jax.ShapeDtypeStruct((count * width, width), jnp.float32),
        ),
        grid_spec=pltpu.PrefetchScalarGridSpec(
            num_scalar_prefetch=1,
            grid=(),
            in_specs=[pl.BlockSpec(memory_space=pl.ANY)],
            out_specs=(memory, memory),
            scratch_shapes=[pltpu.SemaphoreType.DMA((SECTIONS, row_count // width))],
        ),
        compiler_params=pltpu.CompilerParams(vmem_limit_bytes=24 << 20),
    )(order, covariance)


def exchange_kernel(
    planes, x_ref, d_ref, left_ref, right_ref, block_ref, mix, one, two,
    d_pair, d_one, d_two, d_plane, e_pair, e_one, e_two,
    s_pair, r_pair, s_one, r_one, s_two, r_two, s_near, r_near, s_far, r_far, s_mate, r_mate,
    s_up, r_up, s_down, r_down, s_block, r_block, s_plane, r_plane,
):
    z = lax.axis_index("rows")
    me = lax.axis_index("blk")
    last = planes - 1
    chip, core = me // 2, me % 2
    y, x = chip // 2, chip % 2
    across = (y * 2 + 1 - x) * 2 + core
    along = ((1 - y) * 2 + x) * 2 + core
    pair = chip * 2 + 1 - core
    rows = x_ref.shape[4] // CHUNKS

    def lines(c):
        return pl.ds(pl.multiple_of(c * rows, 8), rows)

    def send(src, dst, send_sem, recv_sem, who):
        return pltpu.make_async_remote_copy(
            src_ref=src, dst_ref=dst, send_sem=send_sem, recv_sem=recv_sem,
            device_id=who, device_id_type=MESH,
        )

    def to_pair(c):
        return send(x_ref.at[:, :, :, 1 - core, lines(c)], mix.at[:, :, :, lines(c)],
                    s_pair.at[c], r_pair.at[c], {"blk": pair})

    def first(h, c):
        src = mix.at[0, :, 1 - x, lines(c)] if h == 0 else mix.at[1, 1 - y, :, lines(c)]
        return send(src, one.at[h, :, lines(c)], s_one.at[h, c], r_one.at[h, c], {"blk": along if h else across})

    def second(h, c):
        src = one.at[0, 1 - y, lines(c)] if h == 0 else one.at[1, 1 - x, lines(c)]
        return send(src, two.at[h, lines(c)], s_two.at[h, c], r_two.at[h, c], {"blk": across if h else along})

    def near(h, c):
        here = left_ref.at[:, y, x, core, lines(c)]
        return send(here, here, s_near.at[h, c], r_near.at[h, c], {"blk": along if h else across})

    def far(h, c):
        here = left_ref.at[0, y, 1 - x, core, lines(c)] if h == 0 else left_ref.at[1, 1 - y, x, core, lines(c)]
        return send(here, here, s_far.at[h, c], r_far.at[h, c], {"blk": across if h else along})

    def to_mate(c):
        here = left_ref.at[:, :, :, core, lines(c)]
        return send(here, here, s_mate.at[c], r_mate.at[c], {"blk": pair})

    def up(o, c, step=1):
        here = right_ref.at[o, :, lines(c)]
        return send(here, here, s_up.at[o, c], r_up.at[o, c], {"rows": z + step})

    def down(o, c, step=1):
        here = right_ref.at[o, :, lines(c)]
        return send(here, here, s_down.at[o, c], r_down.at[o, c], {"rows": z - step})

    def block_step(j):
        if j == 0:
            return send(d_ref.at[1 - core], d_pair, s_block.at[0], r_block.at[0], {"blk": pair})
        if j == 1:
            return send(e_pair.at[1 - x], d_one, s_block.at[1], r_block.at[1], {"blk": across})
        if j == 2:
            return send(e_one.at[1 - y], d_two, s_block.at[2], r_block.at[2], {"blk": along})
        here = [block_ref.at[core, x, y], block_ref.at[core, x], block_ref.at[core]][j - 4]
        return send(here, here, s_block.at[j - 1], r_block.at[j - 1], {"blk": [along, across, pair][j - 4]})

    def block_plane(i):
        other = lax.rem(z + i, planes)
        return send(e_two, d_plane.at[i - 1], s_plane.at[i - 1], r_plane.at[i - 1], {"rows": other})

    barrier = pltpu.get_barrier_semaphore()
    for who in (across, along, pair):
        pl.semaphore_signal(barrier, inc=1, device_id={"blk": who}, device_id_type=MESH)
    for i in range(1, planes):
        pl.semaphore_signal(barrier, inc=1, device_id={"rows": lax.rem(z + i, planes)}, device_id_type=MESH)
    pl.semaphore_wait(barrier, 3 + last)

    block_step(0).start()

    def begin(c, carry):
        to_pair(c).start()
        return carry

    lax.fori_loop(0, CHUNKS, begin, 0)

    def when(c, *conditions):
        valid = jnp.logical_and(c >= 0, c < CHUNKS)
        for condition in conditions:
            valid = jnp.logical_and(valid, condition)
        return pl.when(valid)

    def blocks(t):
        @pl.when(t == 0)
        def _():
            block_step(0).wait_recv()
            e_pair[...] = d_ref[core] + d_pair[...]
            block_step(1).start()

        @pl.when(t == 1)
        def _():
            block_step(1).wait_recv()
            e_one[...] = e_pair[x] + d_one[...]
            block_step(2).start()

        @pl.when(t == 2)
        def _():
            block_step(2).wait_recv()
            e_two[...] = e_one[y] + d_two[...]
            for i in range(1, planes):
                block_plane(i).start()

        @pl.when(t == 3)
        def _():
            total = e_two[...]
            for i in range(1, planes):
                block_plane(i).wait_recv()
                total = total + d_plane[i - 1]
            block_ref[core, x, y] = total
            block_step(4).start()

        for j in (4, 5, 6):
            @pl.when(t == j)
            def _():
                block_step(j).wait_recv()
                if j < 6:
                    block_step(j + 1).start()

    def step(t, carry):
        blocks(t)

        c = t

        @when(c)
        def _():
            to_pair(c).wait_recv()
            mix[:, :, :, lines(c)] = mix[:, :, :, lines(c)] + x_ref[:, :, :, core, lines(c)]
            first(0, c).start()
            first(1, c).start()

        c1 = t - 1

        @when(c1)
        def _():
            first(0, c1).wait_recv()
            one[0, :, lines(c1)] = one[0, :, lines(c1)] + mix[0, :, x, lines(c1)]
            second(0, c1).start()
            first(1, c1).wait_recv()
            one[1, :, lines(c1)] = one[1, :, lines(c1)] + mix[1, y, :, lines(c1)]
            second(1, c1).start()

        c2 = t - 2

        @when(c2)
        def _():
            second(0, c2).wait_recv()
            a = one[0, y, lines(c2)] + two[0, lines(c2)]
            left_ref[0, y, x, core, lines(c2)] = a
            right_ref[z, 0, lines(c2)] = a
            second(1, c2).wait_recv()
            b = one[1, x, lines(c2)] + two[1, lines(c2)]
            left_ref[1, y, x, core, lines(c2)] = b
            right_ref[z, 1, lines(c2)] = b

            @pl.when(z < last)
            def _():
                up(z, c2).start()

            @pl.when(z > 0)
            def _():
                down(z, c2).start()

            near(0, c2).start()
            near(1, c2).start()

        for distance in range(1, planes):
            e = t - 2 - HOP * distance

            @when(e, z - distance >= 0)
            def _():
                up(z - distance, e, 0).wait_recv()

                @pl.when(z < last)
                def _():
                    up(z - distance, e).start()

            @when(e, z + distance <= last)
            def _():
                down(z + distance, e, 0).wait_recv()

                @pl.when(z > 0)
                def _():
                    down(z + distance, e).start()

        c3 = t - 4

        @when(c3)
        def _():
            near(0, c3).wait_recv()
            far(0, c3).start()
            near(1, c3).wait_recv()
            far(1, c3).start()

        c4 = t - 6

        @when(c4)
        def _():
            far(0, c4).wait_recv()
            far(1, c4).wait_recv()
            to_mate(c4).start()

        return carry

    lax.fori_loop(0, CHUNKS + max(6, 2 + HOP * last), step, 0)

    for j in (0, 1, 2, 4, 5, 6):
        block_step(j).wait_send()
    for i in range(1, planes):
        block_plane(i).wait_send()

    def finish(c, carry):
        to_mate(c).wait_recv()
        to_pair(c).wait_send()
        to_mate(c).wait_send()
        for h in range(2):
            first(h, c).wait_send()
            second(h, c).wait_send()
            near(h, c).wait_send()
            far(h, c).wait_send()
        for distance in range(planes - 1):
            @pl.when(jnp.logical_and(z - distance >= 0, z < last))
            def _():
                up(z - distance, c).wait_send()

            @pl.when(jnp.logical_and(z + distance <= last, z > 0))
            def _():
                down(z + distance, c).wait_send()

        return carry

    lax.fori_loop(0, CHUNKS, finish, 0)


def exchange(panels, blocks, planes, width):
    depth = panels.shape[1]
    piece = blocks.shape[0] // 8
    dma = pltpu.SemaphoreType.DMA
    memory = pl.BlockSpec(memory_space=pltpu.VMEM)

    def flow(*shape):
        return pltpu.VMEM(shape, jnp.float32)

    return pl.pallas_call(
        functools.partial(exchange_kernel, planes),
        out_shape=(
            jax.ShapeDtypeStruct((2, 2, 2, 2, width, depth), jnp.float32),
            jax.ShapeDtypeStruct((planes, 2, width, depth), jnp.float32),
            jax.ShapeDtypeStruct((2, 2, 2, piece, width), jnp.float32),
        ),
        in_specs=[memory, memory],
        out_specs=(memory, memory, memory),
        scratch_shapes=[
            flow(2, 2, 2, width, depth), flow(2, 2, width, depth), flow(2, width, depth),
            flow(2, 2, piece, width), flow(2, piece, width), flow(piece, width), flow(planes - 1, piece, width),
            flow(2, 2, piece, width), flow(2, piece, width), flow(piece, width),
        ] + [dma((CHUNKS,))] * 2 + [dma((2, CHUNKS))] * 8 + [dma((CHUNKS,))] * 2
        + [dma((planes, CHUNKS))] * 4 + [dma((6,))] * 2 + [dma((planes - 1,))] * 2,
        compiler_params=pltpu.CompilerParams(
            collective_id=0, has_side_effects=True, vmem_limit_bytes=48 << 20
        ),
    )(panels.reshape(2, 2, 2, 2, width, depth), blocks.reshape(2, 2, 2, piece, width))


def product(a, b, dims):
    return lax.dot_general(a, b, (dims, ((), ())), precision=HIGHEST, preferred_element_type=jnp.float32)


def invert_tile(tile):
    size = tile.shape[0]
    row_of = lax.broadcasted_iota(jnp.int32, (size, size), 0)
    column_of = lax.broadcasted_iota(jnp.int32, (size, size), 1)
    right = jnp.where(row_of == column_of, 1.0, 0.0).astype(jnp.float32)
    sub = 8
    left_rows = [tile[i : i + sub] for i in range(0, size, sub)]
    right_rows = [right[i : i + sub] for i in range(0, size, sub)]
    index = lax.broadcasted_iota(jnp.int32, (sub, size), 0)
    scales = [jnp.zeros((sub, size), jnp.float32) for _ in left_rows]
    for k in range(size):
        at, inner = divmod(k, sub)
        pivot = jnp.broadcast_to(left_rows[at][inner : inner + 1, k : k + 1], (1, size))
        scale = 1.0 / pivot
        left_row = left_rows[at][inner : inner + 1, :] * scale
        right_row = right_rows[at][inner : inner + 1, :] * scale
        scales[at] = jnp.where(index == inner, lax.rsqrt(pivot), scales[at])
        for i in range(at, len(left_rows)):
            column = jnp.broadcast_to(left_rows[i][:, k : k + 1], (sub, size))
            if i == at:
                column = jnp.where(index > inner, column, 0.0)
            left_rows[i] = left_rows[i] - column * left_row
            right_rows[i] = right_rows[i] - column * right_row
    return jnp.concatenate([r * s for r, s in zip(right_rows, scales)], axis=0)


def factor_kernel(block_ref, inverse_ref, whole_ref, work, lower, tiles):
    size = work.shape[0]
    width = block_ref.shape[1]
    count = size // TILE
    work[...] = jnp.zeros_like(work)
    block = 0
    for r in range(SECTIONS):
        for c in range(r + 1):
            work[r * width : (r + 1) * width, c * width : (c + 1) * width] = block_ref[block : block + width, :]
            block += width
    inverse_ref[...] = jnp.zeros_like(inverse_ref)

    def one(i, carry):
        at = pl.ds(pl.multiple_of(i * TILE, TILE), TILE)
        tile = invert_tile(work[at, at])
        tiles[i] = tile
        below = product(work[:, at], tile, ((1,), (1,)))
        row_of = lax.broadcasted_iota(jnp.int32, below.shape, 0)
        below = jnp.where(row_of >= (i + 1) * TILE, below, 0.0)
        lower[:, at] = below
        work[...] -= product(below, below, ((1,), (1,)))
        return carry

    lax.fori_loop(0, count, one, 0)
    for i in range(count):
        at = slice(i * TILE, (i + 1) * TILE)
        inverse_ref[at, at] = tiles[i]
        if i:
            done = slice(0, i * TILE)
            seen = product(lower[at, done], inverse_ref[done, done], ((1,), (0,)))
            inverse_ref[at, done] = -product(tiles[i], seen, ((1,), (0,)))
    inverse = inverse_ref[...]
    whole_ref[...] = product(inverse, inverse, ((0,), (0,)))


def factor(block):
    size = SECTIONS * block.shape[1]
    square = jax.ShapeDtypeStruct((size, size), jnp.float32)
    return pl.pallas_call(
        factor_kernel,
        out_shape=(square, square),
        scratch_shapes=[
            pltpu.VMEM((size, size), jnp.float32),
            pltpu.VMEM((size, size), jnp.float32),
            pltpu.VMEM((size // TILE, TILE, TILE), jnp.float32),
        ],
        compiler_params=pltpu.CompilerParams(vmem_limit_bytes=32 << 20),
    )(block)


def update_kernel(order_ref, old_ref, left_ref, right_ref, inverse_ref, whole_ref, out_ref, left_parts, right_parts):
    slots, _, width = right_parts.shape
    rows, depth = left_ref.shape
    lines = old_ref.shape[0] // rows
    halves = width // LANES
    me = lax.axis_index("blk")
    owners = lax.axis_size("blk")

    def matches(section, slot):
        return order_ref[section] == slot * owners + me

    @pl.when(pl.program_id(0) == 0)
    def _():
        def prepare(slot, carry):
            at = pl.ds(pl.multiple_of(slot * width, width), width)
            value = product(whole_ref[...], right_ref[at, :], ((1,), (1,)))
            for section in range(SECTIONS):
                solved = -inverse_ref[section * width : (section + 1) * width, :].T
                value = jnp.where(matches(section, slot), solved, value)
            high, low = split(value)
            right_parts[slot, :depth, :] = high
            right_parts[slot, depth : 2 * depth, :] = low
            right_parts[slot, 2 * depth :, :] = high
            return carry

        lax.fori_loop(0, slots, prepare, 0)

    high, low = split(left_ref[...])
    left_parts[:, :depth] = high
    left_parts[:, depth : 2 * depth] = high
    left_parts[:, 2 * depth :] = low
    for slot in range(slots):
        change = jnp.dot(left_parts[...], right_parts[slot], preferred_element_type=jnp.float32)
        gone = matches(0, slot)
        for section in range(1, SECTIONS):
            gone = jnp.logical_or(gone, matches(section, slot))
        for half in range(halves):
            at = pl.ds(slot * halves + half, rows, stride=lines)
            out_ref[at, :] = jnp.where(gone, 0.0, old_ref[at, :]) - change[:, half * LANES : (half + 1) * LANES]


def update(order, flat, left, right, inverse, whole, width):
    total, depth = left.shape
    rows = min(ROWS, total)
    slots = right.shape[0] // width
    lines = flat.shape[0] // total * rows
    memory = pl.BlockSpec(memory_space=pltpu.VMEM)
    return pl.pallas_call(
        update_kernel,
        out_shape=jax.ShapeDtypeStruct(flat.shape, jnp.float32),
        grid_spec=pltpu.PrefetchScalarGridSpec(
            num_scalar_prefetch=1,
            grid=(total // rows,),
            in_specs=[
                pl.BlockSpec((lines, LANES), lambda i, order: (i, 0)),
                pl.BlockSpec((rows, depth), lambda i, order: (i, 0)),
                memory,
                memory,
                memory,
            ],
            out_specs=pl.BlockSpec((lines, LANES), lambda i, order: (i, 0)),
            scratch_shapes=[
                pltpu.VMEM((rows, 3 * depth), jnp.bfloat16),
                pltpu.VMEM((slots, 3 * depth, width), jnp.bfloat16),
            ],
        ),
        compiler_params=pltpu.CompilerParams(vmem_limit_bytes=56 << 20),
    )(order, flat, left, right, inverse, whole)


def local(covariance, panel_order):
    row_count, slots, _, width = covariance.shape
    owners = lax.axis_size("blk")
    planes = lax.axis_size("rows")
    depth = SECTIONS * width
    row_panels = row_count // width
    panels, blocks = gather(panel_order, covariance)

    if owners == 8 and row_panels == 2 * owners and planes > 1 and SECTIONS == 2 and width % (8 * CHUNKS) == 0:
        left, right, blocks = exchange(panels, blocks, planes, width)
        left = left.reshape(row_count, depth)
        right = right.reshape(slots * width, depth)
        blocks = blocks.reshape(-1, width)
    else:
        targets = [panel_order[section] for section in range(SECTIONS)]
        strips = [
            lax.dynamic_slice_in_dim(covariance, (target % row_panels) * width, width, 0).reshape(width, slots * width)
            for target in targets
        ]
        own = jnp.concatenate(strips, axis=0)
        roots = jnp.stack([target // row_panels for target in targets])
        here = jnp.repeat(roots == lax.axis_index("rows"), width)
        right = lax.psum(jnp.where(here[:, None], own, 0.0), "rows").T
        left = lax.psum(panels, "blk")
        blocks = lax.psum(blocks, ("blk", "rows"))

    inverse, whole = factor(blocks)
    flat = covariance.reshape(row_count * slots * (width // LANES), LANES)
    return update(panel_order, flat, left, right, inverse, whole, width).reshape(covariance.shape)


def solution(mesh):
    return jax.shard_map(
        local,
        mesh=mesh,
        in_specs=(P("rows", None, "blk", None), P()),
        out_specs=P("rows", None, "blk", None),
        check_vma=False,
    )
```

```python
import functools

import jax
import jax.numpy as jnp
from jax import lax
from jax.experimental import pallas as pl
from jax.experimental.pallas import tpu as pltpu
from jax.sharding import PartitionSpec as P

SECTIONS = 2
LANES = 128
CHUNKS = 8
HOP = 1
AHEAD = 2
TILE = 128
SUB = 8
RANK = 8
FACTOR_AT = 3
ROWS = 512
MESH = pl.DeviceIdType.MESH
HIGHEST = lax.Precision.HIGHEST


def split(values):
    high = values.astype(jnp.bfloat16)
    low = (values - high.astype(jnp.float32)).astype(jnp.bfloat16)
    return high, low


def gather_kernel(order_ref, covariance_ref, panels_ref, blocks_ref, sems):
    me = lax.axis_index("blk")
    z = lax.axis_index("rows")
    owners = lax.axis_size("blk")
    row_count, _, _, width = covariance_ref.shape
    row_panels = row_count // width
    targets = [order_ref[section] for section in range(SECTIONS)]
    mine = [lax.rem(target, owners) == me for target in targets]

    def fetch(section, i):
        rows = pl.ds(i * width, width)
        return pltpu.make_async_copy(
            covariance_ref.at[rows, lax.div(targets[section], owners), 0, :],
            panels_ref.at[rows, pl.ds(section * width, width)],
            sems.at[section, i],
        )

    for section in range(SECTIONS):
        @pl.when(mine[section])
        def _():
            for i in range(row_panels):
                fetch(section, i).start()

        @pl.when(jnp.logical_not(mine[section]))
        def _():
            panels_ref[:, section * width : (section + 1) * width] = jnp.zeros((row_count, width), jnp.float32)

    for section in range(SECTIONS):
        @pl.when(mine[section])
        def _():
            for i in range(row_panels):
                fetch(section, i).wait()

    at = 0
    for r in range(SECTIONS):
        for c in range(r + 1):
            root = lax.div(targets[r], row_panels)
            rows = pl.ds(pl.multiple_of(lax.rem(targets[r], row_panels) * width, width), width)
            seen = panels_ref[rows, c * width : (c + 1) * width]
            blocks_ref[at : at + width, :] = jnp.where(root == z, seen, 0.0)
            at += width


def gather(order, covariance):
    row_count, _, _, width = covariance.shape
    count = SECTIONS * (SECTIONS + 1) // 2
    memory = pl.BlockSpec(memory_space=pltpu.VMEM)
    return pl.pallas_call(
        gather_kernel,
        out_shape=(
            jax.ShapeDtypeStruct((row_count, SECTIONS * width), jnp.float32),
            jax.ShapeDtypeStruct((count * width, width), jnp.float32),
        ),
        grid_spec=pltpu.PrefetchScalarGridSpec(
            num_scalar_prefetch=1,
            grid=(),
            in_specs=[pl.BlockSpec(memory_space=pl.ANY)],
            out_specs=(memory, memory),
            scratch_shapes=[pltpu.SemaphoreType.DMA((SECTIONS, row_count // width))],
        ),
        compiler_params=pltpu.CompilerParams(vmem_limit_bytes=24 << 20),
    )(order, covariance)


def product(a, b, dims):
    return lax.dot_general(a, b, (dims, ((), ())), precision=HIGHEST, preferred_element_type=jnp.float32)


def eliminate(left, right, scales, start, count):
    size = left[0].shape[1]
    index = lax.broadcasted_iota(jnp.int32, (SUB, size), 0)
    for k in range(start, start + count, RANK):
        at, inner = divmod(k, SUB)
        entry = [
            [jnp.broadcast_to(left[at][inner + p : inner + p + 1, k + j : k + j + 1], (1, size)) for j in range(RANK)]
            for p in range(RANK)
        ]
        columns = [
            [jnp.broadcast_to(left[i][:, k + j : k + j + 1], (SUB, size)) for j in range(RANK)]
            for i in range(at, len(left))
        ]
        inverse, ratio = [], [[None] * RANK for _ in range(RANK)]
        for p in range(RANK):
            inverse.append(1.0 / entry[p][p])
            scales[at] = jnp.where(index == inner + p, lax.rsqrt(entry[p][p]), scales[at])
            for j in range(p + 1, RANK):
                ratio[j][p] = entry[p][j] * inverse[p]
            for j in range(p + 1, RANK):
                for m in range(j, RANK):
                    entry[j][m] = entry[j][m] - ratio[j][p] * entry[p][m]
        rows = []
        for j in range(RANK):
            l = left[at][inner + j : inner + j + 1, :]
            r = right[at][inner + j : inner + j + 1, :]
            for p in range(j):
                l = l - ratio[j][p] * rows[p][0]
                r = r - ratio[j][p] * rows[p][1]
            rows.append((l, r))
        rows = [(l * inverse[j], r * inverse[j]) for j, (l, r) in enumerate(rows)]
        for i in range(at, len(left)):
            column = columns[i - at]
            for j in range(RANK):
                for p in range(j):
                    column[j] = column[j] - ratio[j][p] * column[p]
            for j in range(RANK):
                c = jnp.where(index > inner + j, column[j], 0.0) if i == at else column[j]
                left[i] = left[i] - c * rows[j][0]
                right[i] = right[i] - c * rows[j][1]


def invert_tile(tile):
    size = tile.shape[0]
    row_of = lax.broadcasted_iota(jnp.int32, (size, size), 0)
    column_of = lax.broadcasted_iota(jnp.int32, (size, size), 1)
    unit = jnp.where(row_of == column_of, 1.0, 0.0).astype(jnp.float32)
    left = [tile[i : i + SUB] for i in range(0, size, SUB)]
    right = [unit[i : i + SUB] for i in range(0, size, SUB)]
    scales = [jnp.zeros((SUB, size), jnp.float32) for _ in left]
    eliminate(left, right, scales, 0, size)
    return jnp.concatenate([r * s for r, s in zip(right, scales)], axis=0)


def factor_tile(i, work, lower, tiles):
    at = pl.ds(pl.multiple_of(i * TILE, TILE), TILE)
    tile = invert_tile(work[at, at])
    tiles[i] = tile
    below = product(work[:, at], tile, ((1,), (1,)))
    row_of = lax.broadcasted_iota(jnp.int32, below.shape, 0)
    below = jnp.where(row_of >= (i + 1) * TILE, below, 0.0)
    lower[:, at] = below
    work[...] -= product(below, below, ((1,), (1,)))


def factor_start(blocks, work):
    width = blocks.shape[1]
    work[...] = jnp.zeros_like(work)
    block = 0
    for r in range(SECTIONS):
        for c in range(r + 1):
            work[r * width : (r + 1) * width, c * width : (c + 1) * width] = blocks[block : block + width, :]
            block += width


def factor_end(lower, tiles, inverse_ref, whole_ref):
    inverse_ref[...] = jnp.zeros_like(inverse_ref)
    for i in range(tiles.shape[0]):
        at = slice(i * TILE, (i + 1) * TILE)
        inverse_ref[at, at] = tiles[i]
        if i:
            done = slice(0, i * TILE)
            seen = product(lower[at, done], inverse_ref[done, done], ((1,), (0,)))
            inverse_ref[at, done] = -product(tiles[i], seen, ((1,), (0,)))
    inverse = inverse_ref[...]
    whole_ref[...] = product(inverse, inverse, ((0,), (0,)))


def factor_scratch(size):
    return [
        pltpu.VMEM((size, size), jnp.float32),
        pltpu.VMEM((size, size), jnp.float32),
        pltpu.VMEM((size // TILE, TILE, TILE), jnp.float32),
        pltpu.VMEM((size, size), jnp.float32),
        pltpu.VMEM((size, size), jnp.float32),
    ]


def prepare(order_ref, slot, cells, inverse_ref, whole_ref, parts_ref):
    width, depth = cells.shape
    me = lax.axis_index("blk")
    owners = lax.axis_size("blk")
    value = product(whole_ref[...], cells, ((1,), (1,)))
    for section in range(SECTIONS):
        solved = -inverse_ref[section * width : (section + 1) * width, :].T
        value = jnp.where(order_ref[section] == slot * owners + me, solved, value)
    high, low = split(value)
    parts_ref[slot, :depth, :] = high
    parts_ref[slot, depth : 2 * depth, :] = low
    parts_ref[slot, 2 * depth :, :] = high


def solve_kernel(order_ref, blocks_ref, cells_ref, parts_ref, work, lower, tiles, inverse, whole):
    width = blocks_ref.shape[1]
    factor_start(blocks_ref[...], work)

    def one(i, carry):
        factor_tile(i, work, lower, tiles)
        return carry

    lax.fori_loop(0, tiles.shape[0], one, 0)
    factor_end(lower, tiles, inverse, whole)
    for slot in range(parts_ref.shape[0]):
        prepare(order_ref, slot, cells_ref[slot * width : (slot + 1) * width, :], inverse, whole, parts_ref)


def solve(order, blocks, cells):
    width = blocks.shape[1]
    depth = SECTIONS * width
    memory = pl.BlockSpec(memory_space=pltpu.VMEM)
    return pl.pallas_call(
        solve_kernel,
        out_shape=jax.ShapeDtypeStruct((cells.shape[0] // width, 3 * depth, width), jnp.bfloat16),
        in_specs=[pl.BlockSpec(memory_space=pltpu.SMEM), memory, memory],
        out_specs=memory,
        scratch_shapes=factor_scratch(depth),
        compiler_params=pltpu.CompilerParams(vmem_limit_bytes=48 << 20),
    )(order, blocks, cells)


def exchange_kernel(
    planes, order_ref, x_ref, d_ref, left_ref, parts_ref, right_ref, block_ref, mix, one, two,
    d_pair, d_one, d_two, d_plane, e_pair, e_one, e_two, diagonal, work, lower, tiles, inverse, whole,
    s_pair, r_pair, s_one, r_one, s_two, r_two, s_near, r_near, s_far, r_far, s_mate, r_mate,
    s_up, r_up, s_down, r_down, s_block, r_block, s_plane, r_plane,
):
    z = lax.axis_index("rows")
    me = lax.axis_index("blk")
    last = planes - 1
    chip, core = me // 2, me % 2
    y, x = chip // 2, chip % 2
    across = (y * 2 + 1 - x) * 2 + core
    along = ((1 - y) * 2 + x) * 2 + core
    pair = chip * 2 + 1 - core
    rows = x_ref.shape[4] // CHUNKS

    def lines(c):
        if c is None:
            return slice(None)
        return pl.ds(pl.multiple_of(c * rows, 8), rows)

    def send(src, dst, send_sem, recv_sem, who):
        return pltpu.make_async_remote_copy(
            src_ref=src, dst_ref=dst, send_sem=send_sem, recv_sem=recv_sem,
            device_id=who, device_id_type=MESH,
        )

    def to_pair(c):
        return send(x_ref.at[:, :, :, 1 - core, lines(c)], mix.at[:, :, :, lines(c)],
                    s_pair.at[0], r_pair.at[0 if c is None else c], {"blk": pair})

    def first(h, c):
        src = mix.at[0, :, 1 - x, lines(c)] if h == 0 else mix.at[1, 1 - y, :, lines(c)]
        return send(src, one.at[h, :, lines(c)], s_one.at[h], r_one.at[h, 0 if c is None else c], {"blk": along if h else across})

    def second(h, c):
        src = one.at[0, 1 - y, lines(c)] if h == 0 else one.at[1, 1 - x, lines(c)]
        return send(src, two.at[h, lines(c)], s_two.at[h], r_two.at[h, 0 if c is None else c], {"blk": across if h else along})

    def near(h, c):
        here = left_ref.at[:, y, x, core, lines(c)]
        return send(here, here, s_near.at[h], r_near.at[h, 0 if c is None else c], {"blk": along if h else across})

    def far(h, c):
        here = left_ref.at[0, y, 1 - x, core, lines(c)] if h == 0 else left_ref.at[1, 1 - y, x, core, lines(c)]
        return send(here, here, s_far.at[h], r_far.at[h, 0 if c is None else c], {"blk": across if h else along})

    def to_mate(c):
        here = left_ref.at[:, :, :, core, lines(c)]
        return send(here, here, s_mate.at[0], r_mate.at[0], {"blk": pair})

    def up(o, c, step=1):
        here = right_ref.at[o, :, lines(c)]
        return send(here, here, s_up.at[o], r_up.at[o, 0 if c is None else c], {"rows": z + step})

    def down(o, c, step=1):
        here = right_ref.at[o, :, lines(c)]
        return send(here, here, s_down.at[o], r_down.at[o, 0 if c is None else c], {"rows": z - step})

    def block_step(j):
        if j == 0:
            return send(d_ref.at[1 - core], d_pair, s_block.at[0], r_block.at[0], {"blk": pair})
        if j == 1:
            return send(e_pair.at[1 - x], d_one, s_block.at[1], r_block.at[1], {"blk": across})
        if j == 2:
            return send(e_one.at[1 - y], d_two, s_block.at[2], r_block.at[2], {"blk": along})
        here = [block_ref.at[core, x, y], block_ref.at[core, x], block_ref.at[core]][j - 4]
        return send(here, here, s_block.at[j - 1], r_block.at[j - 1], {"blk": [along, across, pair][j - 4]})

    def block_plane(i):
        other = lax.rem(z + i, planes)
        return send(e_two, d_plane.at[i - 1], s_plane.at[i - 1], r_plane.at[i - 1], {"rows": other})

    barrier = pltpu.get_barrier_semaphore()
    for who in (across, along, pair):
        pl.semaphore_signal(barrier, inc=1, device_id={"blk": who}, device_id_type=MESH)
    for i in range(1, planes):
        pl.semaphore_signal(barrier, inc=1, device_id={"rows": lax.rem(z + i, planes)}, device_id_type=MESH)
    pl.semaphore_wait(barrier, 3 + last)

    block_step(0).start()

    def begin(c, carry):
        to_pair(c).start()
        return carry

    lax.fori_loop(0, AHEAD, begin, 0)

    def when(c, *conditions):
        valid = jnp.logical_and(c >= 0, c < CHUNKS)
        for condition in conditions:
            valid = jnp.logical_and(valid, condition)
        return pl.when(valid)

    def blocks(j):
        if j == 0:
            block_step(0).wait_recv()
            e_pair[...] = d_ref[core] + d_pair[...]
            block_step(1).start()
        elif j == 1:
            block_step(1).wait_recv()
            e_one[...] = e_pair[x] + d_one[...]
            block_step(2).start()
        elif j == 2:
            block_step(2).wait_recv()
            e_two[...] = e_one[y] + d_two[...]
            for i in range(1, planes):
                block_plane(i).start()
        elif j == 3:
            total = e_two[...]
            for i in range(1, planes):
                block_plane(i).wait_recv()
                total = total + d_plane[i - 1]
            block_ref[core, x, y] = total
            block_step(4).start()
        else:
            block_step(j).wait_recv()
            if j < 6:
                block_step(j + 1).start()

    def block_stages(t, which):
        for j in range(which, 7, 2):
            @pl.when(t == j // 2)
            def _():
                blocks(j)

    def factor_stages(t):
        count = tiles.shape[0]
        piece = block_ref.shape[3]

        @pl.when(t == FACTOR_AT)
        def _():
            for k in range(8):
                diagonal[k * piece : (k + 1) * piece, :] = block_ref[k // 4, k // 2 % 2, k % 2]
            factor_start(diagonal[...], work)

        @pl.when(jnp.logical_and(t >= FACTOR_AT, t < FACTOR_AT + count))
        def _():
            factor_tile(t - FACTOR_AT, work, lower, tiles)

        @pl.when(t == FACTOR_AT + count)
        def _():
            factor_end(lower, tiles, inverse, whole)

    def solve_cells(o):
        for h in range(2):
            prepare(order_ref, 2 * o + h, right_ref[o, h], inverse, whole, parts_ref)

    def step(t, carry):
        block_stages(t, 0)
        c = t

        @when(c)
        def _():
            to_pair(c).wait_recv()

            @pl.when(c + AHEAD < CHUNKS)
            def _():
                to_pair(c + AHEAD).start()

            mix[:, :, :, lines(c)] = mix[:, :, :, lines(c)] + x_ref[:, :, :, core, lines(c)]
            first(0, c).start()
            first(1, c).start()

        block_stages(t, 1)
        c1 = t - 1

        @when(c1)
        def _():
            first(0, c1).wait_recv()
            one[0, :, lines(c1)] = one[0, :, lines(c1)] + mix[0, :, x, lines(c1)]
            second(0, c1).start()
            first(1, c1).wait_recv()
            one[1, :, lines(c1)] = one[1, :, lines(c1)] + mix[1, y, :, lines(c1)]
            second(1, c1).start()

        c2 = t - 2

        @when(c2)
        def _():
            second(0, c2).wait_recv()
            a = one[0, y, lines(c2)] + two[0, lines(c2)]
            left_ref[0, y, x, core, lines(c2)] = a
            right_ref[z, 0, lines(c2)] = a
            second(1, c2).wait_recv()
            b = one[1, x, lines(c2)] + two[1, lines(c2)]
            left_ref[1, y, x, core, lines(c2)] = b
            right_ref[z, 1, lines(c2)] = b

            @pl.when(z < last)
            def _():
                up(z, c2).start()

            @pl.when(z > 0)
            def _():
                down(z, c2).start()

            near(0, c2).start()
            near(1, c2).start()

        for distance in range(1, planes):
            e = t - 2 - HOP * distance

            @when(e, z - distance >= 0)
            def _():
                up(z - distance, e, 0).wait_recv()

                @pl.when(z < last)
                def _():
                    up(z - distance, e).start()

            @when(e, z + distance <= last)
            def _():
                down(z + distance, e, 0).wait_recv()

                @pl.when(z > 0)
                def _():
                    down(z + distance, e).start()

        c3 = t - 4

        @when(c3)
        def _():
            near(0, c3).wait_recv()
            far(0, c3).start()
            near(1, c3).wait_recv()
            far(1, c3).start()

        c4 = t - 6

        @when(c4)
        def _():
            far(0, c4).wait_recv()
            far(1, c4).wait_recv()
            to_mate(c4).start()

        factor_stages(t)

        for distance in range(planes):
            now = t == CHUNKS + max(FACTOR_AT + 5 - CHUNKS, 1 + HOP * distance)

            @pl.when(jnp.logical_and(now, z - distance >= 0))
            def _():
                solve_cells(z - distance)

            if distance:
                @pl.when(jnp.logical_and(now, z + distance <= last))
                def _():
                    solve_cells(z + distance)

        return carry

    lax.fori_loop(0, CHUNKS + max(6, 2 + HOP * last), step, 0)
    to_mate(None).wait_recv()
    for j in (0, 1, 2, 4, 5, 6):
        block_step(j).wait_send()
    for i in range(1, planes):
        block_plane(i).wait_send()
    to_pair(None).wait_send()
    to_mate(None).wait_send()
    for h in range(2):
        first(h, None).wait_send()
        second(h, None).wait_send()
        near(h, None).wait_send()
        far(h, None).wait_send()
    for distance in range(planes - 1):
        @pl.when(jnp.logical_and(z - distance >= 0, z < last))
        def _():
            up(z - distance, None).wait_send()

        @pl.when(jnp.logical_and(z + distance <= last, z > 0))
        def _():
            down(z + distance, None).wait_send()


def exchange(order, panels, blocks, planes, width):
    depth = panels.shape[1]
    piece = blocks.shape[0] // 8
    dma = pltpu.SemaphoreType.DMA
    memory = pl.BlockSpec(memory_space=pltpu.VMEM)

    def flow(*shape):
        return pltpu.VMEM(shape, jnp.float32)

    return pl.pallas_call(
        functools.partial(exchange_kernel, planes),
        out_shape=(
            jax.ShapeDtypeStruct((2, 2, 2, 2, width, depth), jnp.float32),
            jax.ShapeDtypeStruct((2 * planes, 3 * depth, width), jnp.bfloat16),
        ),
        in_specs=[pl.BlockSpec(memory_space=pltpu.SMEM), memory, memory],
        out_specs=(memory, memory),
        scratch_shapes=[
            flow(planes, 2, width, depth), flow(2, 2, 2, piece, width),
            flow(2, 2, 2, width, depth), flow(2, 2, width, depth), flow(2, width, depth),
            flow(2, 2, piece, width), flow(2, piece, width), flow(piece, width), flow(planes - 1, piece, width),
            flow(2, 2, piece, width), flow(2, piece, width), flow(piece, width), flow(8 * piece, width),
        ] + factor_scratch(depth)
        + [dma((1,)), dma((CHUNKS,))] + [dma((2,)), dma((2, CHUNKS))] * 4 + [dma((1,))] * 2
        + [dma((planes,)), dma((planes, CHUNKS))] * 2 + [dma((6,))] * 2 + [dma((planes - 1,))] * 2,
        compiler_params=pltpu.CompilerParams(
            collective_id=0, has_side_effects=True, vmem_limit_bytes=56 << 20
        ),
    )(order, panels.reshape(2, 2, 2, 2, width, depth), blocks.reshape(2, 2, 2, piece, width))


def update_kernel(order_ref, old_ref, left_ref, parts_ref, out_ref, left_parts):
    slots, _, width = parts_ref.shape
    rows, depth = left_ref.shape
    lines = old_ref.shape[0] // rows
    halves = width // LANES
    me = lax.axis_index("blk")
    owners = lax.axis_size("blk")

    def matches(section, slot):
        return order_ref[section] == slot * owners + me

    high, low = split(left_ref[...])
    left_parts[:, :depth] = high
    left_parts[:, depth : 2 * depth] = high
    left_parts[:, 2 * depth :] = low
    for slot in range(slots):
        change = jnp.dot(left_parts[...], parts_ref[slot], preferred_element_type=jnp.float32)
        gone = matches(0, slot)
        for section in range(1, SECTIONS):
            gone = jnp.logical_or(gone, matches(section, slot))
        for half in range(halves):
            at = pl.ds(slot * halves + half, rows, stride=lines)
            out_ref[at, :] = jnp.where(gone, 0.0, old_ref[at, :]) - change[:, half * LANES : (half + 1) * LANES]


def update(order, flat, left, parts):
    total, depth = left.shape
    rows = min(ROWS, total)
    lines = flat.shape[0] // total * rows
    memory = pl.BlockSpec(memory_space=pltpu.VMEM)
    return pl.pallas_call(
        update_kernel,
        out_shape=jax.ShapeDtypeStruct(flat.shape, jnp.float32),
        grid_spec=pltpu.PrefetchScalarGridSpec(
            num_scalar_prefetch=1,
            grid=(total // rows,),
            in_specs=[
                pl.BlockSpec((lines, LANES), lambda i, order: (i, 0)),
                pl.BlockSpec((rows, depth), lambda i, order: (i, 0)),
                memory,
            ],
            out_specs=pl.BlockSpec((lines, LANES), lambda i, order: (i, 0)),
            scratch_shapes=[pltpu.VMEM((rows, 3 * depth), jnp.bfloat16)],
        ),
        compiler_params=pltpu.CompilerParams(vmem_limit_bytes=56 << 20),
    )(order, flat, left, parts)


def local(covariance, panel_order):
    row_count, slots, _, width = covariance.shape
    owners = lax.axis_size("blk")
    planes = lax.axis_size("rows")
    depth = SECTIONS * width
    row_panels = row_count // width
    panels, blocks = gather(panel_order, covariance)

    if owners == 8 and row_panels == 2 * owners and planes > 1 and SECTIONS == 2 and width % (8 * CHUNKS) == 0:
        left, parts = exchange(panel_order, panels, blocks, planes, width)
        left = left.reshape(row_count, depth)
    else:
        targets = [panel_order[section] for section in range(SECTIONS)]
        strips = [
            lax.dynamic_slice_in_dim(covariance, (target % row_panels) * width, width, 0).reshape(width, slots * width)
            for target in targets
        ]
        own = jnp.concatenate(strips, axis=0)
        roots = jnp.stack([target // row_panels for target in targets])
        here = jnp.repeat(roots == lax.axis_index("rows"), width)
        right = lax.psum(jnp.where(here[:, None], own, 0.0), "rows").T
        left = lax.psum(panels, "blk")
        parts = solve(panel_order, lax.psum(blocks, ("blk", "rows")), right)

    flat = covariance.reshape(row_count * slots * (width // LANES), LANES)
    return update(panel_order, flat, left, parts).reshape(covariance.shape)


def solution(mesh):
    return jax.shard_map(
        local,
        mesh=mesh,
        in_specs=(P("rows", None, "blk", None), P()),
        out_specs=P("rows", None, "blk", None),
        check_vma=False,
    )
```

```python
import functools

import jax
import jax.numpy as jnp
from jax import lax
from jax.experimental import pallas as pl
from jax.experimental.pallas import tpu as pltpu
from jax.sharding import PartitionSpec as P

SECTIONS = 2
LANES = 128
CHUNKS = 8
HOP = 1
AHEAD = 2
TILE = 128
SUB = 8
RANK = 8
FACTOR_AT = 6
ROWS = 256
MESH = pl.DeviceIdType.MESH
HIGHEST = lax.Precision.HIGHEST


def split(values):
    high = values.astype(jnp.bfloat16)
    low = (values - high.astype(jnp.float32)).astype(jnp.bfloat16)
    return high, low


def gather_kernel(order_ref, covariance_ref, panels_ref, blocks_ref, sems):
    me = lax.axis_index("blk")
    z = lax.axis_index("rows")
    owners = lax.axis_size("blk")
    row_count, _, _, width = covariance_ref.shape
    row_panels = row_count // width
    targets = [order_ref[section] for section in range(SECTIONS)]
    mine = [lax.rem(target, owners) == me for target in targets]

    def fetch(section, i):
        rows = pl.ds(i * width, width)
        return pltpu.make_async_copy(
            covariance_ref.at[rows, lax.div(targets[section], owners), 0, :],
            panels_ref.at[rows, pl.ds(section * width, width)],
            sems.at[section, i],
        )

    for section in range(SECTIONS):
        @pl.when(mine[section])
        def _():
            for i in range(row_panels):
                fetch(section, i).start()

        @pl.when(jnp.logical_not(mine[section]))
        def _():
            panels_ref[:, section * width : (section + 1) * width] = jnp.zeros((row_count, width), jnp.float32)

    for section in range(SECTIONS):
        @pl.when(mine[section])
        def _():
            for i in range(row_panels):
                fetch(section, i).wait()

    at = 0
    for r in range(SECTIONS):
        for c in range(r + 1):
            root = lax.div(targets[r], row_panels)
            rows = pl.ds(pl.multiple_of(lax.rem(targets[r], row_panels) * width, width), width)
            seen = panels_ref[rows, c * width : (c + 1) * width]
            blocks_ref[at : at + width, :] = jnp.where(root == z, seen, 0.0)
            at += width


def gather(order, covariance):
    row_count, _, _, width = covariance.shape
    count = SECTIONS * (SECTIONS + 1) // 2
    memory = pl.BlockSpec(memory_space=pltpu.VMEM)
    return pl.pallas_call(
        gather_kernel,
        out_shape=(
            jax.ShapeDtypeStruct((row_count, SECTIONS * width), jnp.float32),
            jax.ShapeDtypeStruct((count * width, width), jnp.float32),
        ),
        grid_spec=pltpu.PrefetchScalarGridSpec(
            num_scalar_prefetch=1,
            grid=(),
            in_specs=[pl.BlockSpec(memory_space=pl.ANY)],
            out_specs=(memory, memory),
            scratch_shapes=[pltpu.SemaphoreType.DMA((SECTIONS, row_count // width))],
        ),
        compiler_params=pltpu.CompilerParams(vmem_limit_bytes=24 << 20),
    )(order, covariance)


def product(a, b, dims):
    return lax.dot_general(a, b, (dims, ((), ())), precision=HIGHEST, preferred_element_type=jnp.float32)


def eliminate(left, right, scales, start, count):
    size = left[0].shape[1]
    index = lax.broadcasted_iota(jnp.int32, (SUB, size), 0)
    for k in range(start, start + count, RANK):
        at, inner = divmod(k, SUB)
        entry = [
            [jnp.broadcast_to(left[at][inner + p : inner + p + 1, k + j : k + j + 1], (1, size)) for j in range(RANK)]
            for p in range(RANK)
        ]
        columns = [
            [jnp.broadcast_to(left[i][:, k + j : k + j + 1], (SUB, size)) for j in range(RANK)]
            for i in range(at, len(left))
        ]
        inverse, ratio = [], [[None] * RANK for _ in range(RANK)]
        for p in range(RANK):
            inverse.append(1.0 / entry[p][p])
            scales[at] = jnp.where(index == inner + p, lax.rsqrt(entry[p][p]), scales[at])
            for j in range(p + 1, RANK):
                ratio[j][p] = entry[p][j] * inverse[p]
            for j in range(p + 1, RANK):
                for m in range(j, RANK):
                    entry[j][m] = entry[j][m] - ratio[j][p] * entry[p][m]
        rows = []
        for j in range(RANK):
            l = left[at][inner + j : inner + j + 1, :]
            r = right[at][inner + j : inner + j + 1, :]
            for p in range(j):
                l = l - ratio[j][p] * rows[p][0]
                r = r - ratio[j][p] * rows[p][1]
            rows.append((l, r))
        rows = [(l * inverse[j], r * inverse[j]) for j, (l, r) in enumerate(rows)]
        for i in range(at, len(left)):
            column = columns[i - at]
            for j in range(RANK):
                for p in range(j):
                    column[j] = column[j] - ratio[j][p] * column[p]
            for j in range(RANK):
                c = jnp.where(index > inner + j, column[j], 0.0) if i == at else column[j]
                left[i] = left[i] - c * rows[j][0]
                right[i] = right[i] - c * rows[j][1]


def invert_tile(tile):
    size = tile.shape[0]
    row_of = lax.broadcasted_iota(jnp.int32, (size, size), 0)
    column_of = lax.broadcasted_iota(jnp.int32, (size, size), 1)
    unit = jnp.where(row_of == column_of, 1.0, 0.0).astype(jnp.float32)
    left = [tile[i : i + SUB] for i in range(0, size, SUB)]
    right = [unit[i : i + SUB] for i in range(0, size, SUB)]
    scales = [jnp.zeros((SUB, size), jnp.float32) for _ in left]
    eliminate(left, right, scales, 0, size)
    return jnp.concatenate([r * s for r, s in zip(right, scales)], axis=0)


def factor_tile(i, work, lower, tiles):
    at = pl.ds(pl.multiple_of(i * TILE, TILE), TILE)
    tile = invert_tile(work[at, at])
    tiles[i] = tile
    below = product(work[:, at], tile, ((1,), (1,)))
    row_of = lax.broadcasted_iota(jnp.int32, below.shape, 0)
    below = jnp.where(row_of >= (i + 1) * TILE, below, 0.0)
    lower[:, at] = below
    work[...] -= product(below, below, ((1,), (1,)))


def factor_start(blocks, work):
    width = blocks.shape[1]
    work[...] = jnp.zeros_like(work)
    block = 0
    for r in range(SECTIONS):
        for c in range(r + 1):
            work[r * width : (r + 1) * width, c * width : (c + 1) * width] = blocks[block : block + width, :]
            block += width


def factor_end(lower, tiles, inverse_ref, whole_ref):
    inverse_ref[...] = jnp.zeros_like(inverse_ref)
    for i in range(tiles.shape[0]):
        at = slice(i * TILE, (i + 1) * TILE)
        inverse_ref[at, at] = tiles[i]
        if i:
            done = slice(0, i * TILE)
            seen = product(lower[at, done], inverse_ref[done, done], ((1,), (0,)))
            inverse_ref[at, done] = -product(tiles[i], seen, ((1,), (0,)))
    inverse = inverse_ref[...]
    whole_ref[...] = product(inverse, inverse, ((0,), (0,)))


def factor_scratch(size):
    return [
        pltpu.VMEM((size, size), jnp.float32),
        pltpu.VMEM((size, size), jnp.float32),
        pltpu.VMEM((size // TILE, TILE, TILE), jnp.float32),
        pltpu.VMEM((size, size), jnp.float32),
        pltpu.VMEM((size, size), jnp.float32),
    ]


def prepare(order_ref, slot, cells, inverse_ref, whole_ref, parts_ref):
    width, depth = cells.shape
    me = lax.axis_index("blk")
    owners = lax.axis_size("blk")
    value = product(whole_ref[...], cells, ((1,), (1,)))
    for section in range(SECTIONS):
        solved = -inverse_ref[section * width : (section + 1) * width, :].T
        value = jnp.where(order_ref[section] == slot * owners + me, solved, value)
    high, low = split(value)
    parts_ref[slot, :depth, :] = high
    parts_ref[slot, depth : 2 * depth, :] = low
    parts_ref[slot, 2 * depth :, :] = high


def solve_kernel(order_ref, blocks_ref, cells_ref, parts_ref, work, lower, tiles, inverse, whole):
    width = blocks_ref.shape[1]
    factor_start(blocks_ref[...], work)

    def one(i, carry):
        factor_tile(i, work, lower, tiles)
        return carry

    lax.fori_loop(0, tiles.shape[0], one, 0)
    factor_end(lower, tiles, inverse, whole)
    for slot in range(parts_ref.shape[0]):
        prepare(order_ref, slot, cells_ref[slot * width : (slot + 1) * width, :], inverse, whole, parts_ref)


def solve(order, blocks, cells):
    width = blocks.shape[1]
    depth = SECTIONS * width
    memory = pl.BlockSpec(memory_space=pltpu.VMEM)
    return pl.pallas_call(
        solve_kernel,
        out_shape=jax.ShapeDtypeStruct((cells.shape[0] // width, 3 * depth, width), jnp.bfloat16),
        in_specs=[pl.BlockSpec(memory_space=pltpu.SMEM), memory, memory],
        out_specs=memory,
        scratch_shapes=factor_scratch(depth),
        compiler_params=pltpu.CompilerParams(vmem_limit_bytes=48 << 20),
    )(order, blocks, cells)


def exchange_kernel(
    planes, order_ref, x_ref, d_ref, left_ref, parts_ref, right_ref, block_ref, mix, one, two,
    d_pair, d_one, d_two, d_plane, e_pair, e_one, e_two, diagonal, work, lower, tiles, inverse, whole,
    s_pair, r_pair, s_one, r_one, s_two, r_two, s_near, r_near, s_far, r_far, s_mate, r_mate,
    s_up, r_up, s_down, r_down, s_block, r_block, s_plane, r_plane,
):
    z = lax.axis_index("rows")
    me = lax.axis_index("blk")
    last = planes - 1
    chip, core = me // 2, me % 2
    y, x = chip // 2, chip % 2
    across = (y * 2 + 1 - x) * 2 + core
    along = ((1 - y) * 2 + x) * 2 + core
    pair = chip * 2 + 1 - core
    rows = x_ref.shape[4] // CHUNKS

    def lines(c):
        if c is None:
            return slice(None)
        return pl.ds(pl.multiple_of(c * rows, 8), rows)

    def send(src, dst, send_sem, recv_sem, who):
        return pltpu.make_async_remote_copy(
            src_ref=src, dst_ref=dst, send_sem=send_sem, recv_sem=recv_sem,
            device_id=who, device_id_type=MESH,
        )

    def to_pair(c):
        return send(x_ref.at[:, :, :, 1 - core, lines(c)], mix.at[:, :, :, lines(c)],
                    s_pair.at[0], r_pair.at[0 if c is None else c], {"blk": pair})

    def first(h, c):
        src = mix.at[0, :, 1 - x, lines(c)] if h == 0 else mix.at[1, 1 - y, :, lines(c)]
        return send(src, one.at[h, :, lines(c)], s_one.at[h], r_one.at[h, 0 if c is None else c], {"blk": along if h else across})

    def second(h, c):
        src = one.at[0, 1 - y, lines(c)] if h == 0 else one.at[1, 1 - x, lines(c)]
        return send(src, two.at[h, lines(c)], s_two.at[h], r_two.at[h, 0 if c is None else c], {"blk": across if h else along})

    def near(h, c):
        here = left_ref.at[:, y, x, core, lines(c)]
        return send(here, here, s_near.at[h], r_near.at[h, 0 if c is None else c], {"blk": along if h else across})

    def far(h, c):
        here = left_ref.at[0, y, 1 - x, core, lines(c)] if h == 0 else left_ref.at[1, 1 - y, x, core, lines(c)]
        return send(here, here, s_far.at[h], r_far.at[h, 0 if c is None else c], {"blk": across if h else along})

    def to_mate(c):
        here = left_ref.at[:, :, :, core, lines(c)]
        return send(here, here, s_mate.at[0], r_mate.at[0], {"blk": pair})

    def up(o, c, step=1):
        here = right_ref.at[o, :, lines(c)]
        return send(here, here, s_up.at[o], r_up.at[o, 0 if c is None else c], {"rows": z + step})

    def down(o, c, step=1):
        here = right_ref.at[o, :, lines(c)]
        return send(here, here, s_down.at[o], r_down.at[o, 0 if c is None else c], {"rows": z - step})

    def block_step(j):
        if j == 0:
            return send(d_ref.at[1 - core], d_pair, s_block.at[0], r_block.at[0], {"blk": pair})
        if j == 1:
            return send(e_pair.at[1 - x], d_one, s_block.at[1], r_block.at[1], {"blk": across})
        if j == 2:
            return send(e_one.at[1 - y], d_two, s_block.at[2], r_block.at[2], {"blk": along})
        here = [block_ref.at[core, x, y], block_ref.at[core, x], block_ref.at[core]][j - 4]
        return send(here, here, s_block.at[j - 1], r_block.at[j - 1], {"blk": [along, across, pair][j - 4]})

    def block_plane(i):
        other = lax.rem(z + i, planes)
        return send(e_two, d_plane.at[i - 1], s_plane.at[i - 1], r_plane.at[i - 1], {"rows": other})

    barrier = pltpu.get_barrier_semaphore()
    for who in (across, along, pair):
        pl.semaphore_signal(barrier, inc=1, device_id={"blk": who}, device_id_type=MESH)
    for i in range(1, planes):
        pl.semaphore_signal(barrier, inc=1, device_id={"rows": lax.rem(z + i, planes)}, device_id_type=MESH)
    pl.semaphore_wait(barrier, 3 + last)

    block_step(0).start()

    def begin(c, carry):
        to_pair(c).start()
        return carry

    lax.fori_loop(0, AHEAD, begin, 0)

    def when(c, *conditions):
        valid = jnp.logical_and(c >= 0, c < CHUNKS)
        for condition in conditions:
            valid = jnp.logical_and(valid, condition)
        return pl.when(valid)

    def blocks(j):
        if j == 0:
            block_step(0).wait_recv()
            e_pair[...] = d_ref[core] + d_pair[...]
            block_step(1).start()
        elif j == 1:
            block_step(1).wait_recv()
            e_one[...] = e_pair[x] + d_one[...]
            block_step(2).start()
        elif j == 2:
            block_step(2).wait_recv()
            e_two[...] = e_one[y] + d_two[...]
            for i in range(1, planes):
                block_plane(i).start()
        elif j == 3:
            total = e_two[...]
            for i in range(1, planes):
                block_plane(i).wait_recv()
                total = total + d_plane[i - 1]
            block_ref[core, x, y] = total
            block_step(4).start()
        else:
            block_step(j).wait_recv()
            if j < 6:
                block_step(j + 1).start()

    def block_stages(t):
        for j in range(7):
            @pl.when(t == j)
            def _():
                blocks(j)

    def factor_stages(t):
        count = tiles.shape[0]
        piece = block_ref.shape[3]

        @pl.when(t == FACTOR_AT)
        def _():
            for k in range(8):
                diagonal[k * piece : (k + 1) * piece, :] = block_ref[k // 4, k // 2 % 2, k % 2]
            factor_start(diagonal[...], work)

        @pl.when(jnp.logical_and(t >= FACTOR_AT, t < FACTOR_AT + count))
        def _():
            factor_tile(t - FACTOR_AT, work, lower, tiles)

        @pl.when(t == FACTOR_AT + count)
        def _():
            factor_end(lower, tiles, inverse, whole)

    def solve_cells(o):
        for h in range(2):
            prepare(order_ref, 2 * o + h, right_ref[o, h], inverse, whole, parts_ref)

    def step(t, carry):
        block_stages(t)
        c = t

        @when(c)
        def _():
            to_pair(c).wait_recv()

            @pl.when(c + AHEAD < CHUNKS)
            def _():
                to_pair(c + AHEAD).start()

            mix[:, :, :, lines(c)] = mix[:, :, :, lines(c)] + x_ref[:, :, :, core, lines(c)]
            first(0, c).start()
            first(1, c).start()

        c1 = t - 1

        @when(c1)
        def _():
            first(0, c1).wait_recv()
            one[0, :, lines(c1)] = one[0, :, lines(c1)] + mix[0, :, x, lines(c1)]
            second(0, c1).start()
            first(1, c1).wait_recv()
            one[1, :, lines(c1)] = one[1, :, lines(c1)] + mix[1, y, :, lines(c1)]
            second(1, c1).start()

        c2 = t - 2

        @when(c2)
        def _():
            second(0, c2).wait_recv()
            a = one[0, y, lines(c2)] + two[0, lines(c2)]
            left_ref[0, y, x, core, lines(c2)] = a
            right_ref[z, 0, lines(c2)] = a
            second(1, c2).wait_recv()
            b = one[1, x, lines(c2)] + two[1, lines(c2)]
            left_ref[1, y, x, core, lines(c2)] = b
            right_ref[z, 1, lines(c2)] = b

            @pl.when(z < last)
            def _():
                up(z, c2).start()

            @pl.when(z > 0)
            def _():
                down(z, c2).start()

            near(0, c2).start()
            near(1, c2).start()

        for distance in range(1, planes):
            e = t - 2 - HOP * distance

            @when(e, z - distance >= 0)
            def _():
                up(z - distance, e, 0).wait_recv()

                @pl.when(z < last)
                def _():
                    up(z - distance, e).start()

            @when(e, z + distance <= last)
            def _():
                down(z + distance, e, 0).wait_recv()

                @pl.when(z > 0)
                def _():
                    down(z + distance, e).start()

        c3 = t - 4

        @when(c3)
        def _():
            near(0, c3).wait_recv()
            far(0, c3).start()
            near(1, c3).wait_recv()
            far(1, c3).start()

        c4 = t - 6

        @when(c4)
        def _():
            far(0, c4).wait_recv()
            far(1, c4).wait_recv()
            to_mate(c4).start()

        factor_stages(t)

        for distance in range(planes):
            now = t == CHUNKS + max(FACTOR_AT + 5 - CHUNKS, 1 + HOP * distance)

            @pl.when(jnp.logical_and(now, z - distance >= 0))
            def _():
                solve_cells(z - distance)

            if distance:
                @pl.when(jnp.logical_and(now, z + distance <= last))
                def _():
                    solve_cells(z + distance)

        return carry

    lax.fori_loop(0, CHUNKS + max(6, 2 + HOP * last), step, 0)
    to_mate(None).wait_recv()
    for j in (0, 1, 2, 4, 5, 6):
        block_step(j).wait_send()
    for i in range(1, planes):
        block_plane(i).wait_send()
    to_pair(None).wait_send()
    to_mate(None).wait_send()
    for h in range(2):
        first(h, None).wait_send()
        second(h, None).wait_send()
        near(h, None).wait_send()
        far(h, None).wait_send()
    for distance in range(planes - 1):
        @pl.when(jnp.logical_and(z - distance >= 0, z < last))
        def _():
            up(z - distance, None).wait_send()

        @pl.when(jnp.logical_and(z + distance <= last, z > 0))
        def _():
            down(z + distance, None).wait_send()


def exchange(order, panels, blocks, planes, width):
    depth = panels.shape[1]
    piece = blocks.shape[0] // 8
    dma = pltpu.SemaphoreType.DMA
    memory = pl.BlockSpec(memory_space=pltpu.VMEM)

    def flow(*shape):
        return pltpu.VMEM(shape, jnp.float32)

    return pl.pallas_call(
        functools.partial(exchange_kernel, planes),
        out_shape=(
            jax.ShapeDtypeStruct((2, 2, 2, 2, width, depth), jnp.float32),
            jax.ShapeDtypeStruct((2 * planes, 3 * depth, width), jnp.bfloat16),
        ),
        in_specs=[pl.BlockSpec(memory_space=pltpu.SMEM), memory, memory],
        out_specs=(memory, memory),
        scratch_shapes=[
            flow(planes, 2, width, depth), flow(2, 2, 2, piece, width),
            flow(2, 2, 2, width, depth), flow(2, 2, width, depth), flow(2, width, depth),
            flow(2, 2, piece, width), flow(2, piece, width), flow(piece, width), flow(planes - 1, piece, width),
            flow(2, 2, piece, width), flow(2, piece, width), flow(piece, width), flow(8 * piece, width),
        ] + factor_scratch(depth)
        + [dma((1,)), dma((CHUNKS,))] + [dma((2,)), dma((2, CHUNKS))] * 4 + [dma((1,))] * 2
        + [dma((planes,)), dma((planes, CHUNKS))] * 2 + [dma((6,))] * 2 + [dma((planes - 1,))] * 2,
        compiler_params=pltpu.CompilerParams(
            collective_id=0, has_side_effects=True, vmem_limit_bytes=56 << 20
        ),
    )(order, panels.reshape(2, 2, 2, 2, width, depth), blocks.reshape(2, 2, 2, piece, width))


def update_kernel(order_ref, old_ref, left_ref, parts_ref, out_ref, left_parts):
    slots, _, width = parts_ref.shape
    rows, depth = left_ref.shape
    lines = old_ref.shape[0] // rows
    halves = width // LANES
    me = lax.axis_index("blk")
    owners = lax.axis_size("blk")

    def matches(section, slot):
        return order_ref[section] == slot * owners + me

    high, low = split(left_ref[...])
    left_parts[:, :depth] = high
    left_parts[:, depth : 2 * depth] = high
    left_parts[:, 2 * depth :] = low
    for slot in range(slots):
        change = jnp.dot(left_parts[...], parts_ref[slot], preferred_element_type=jnp.float32)
        gone = matches(0, slot)
        for section in range(1, SECTIONS):
            gone = jnp.logical_or(gone, matches(section, slot))
        for half in range(halves):
            at = pl.ds(slot * halves + half, rows, stride=lines)
            out_ref[at, :] = jnp.where(gone, 0.0, old_ref[at, :]) - change[:, half * LANES : (half + 1) * LANES]


def update(order, flat, left, parts):
    total, depth = left.shape
    rows = min(ROWS, total)
    lines = flat.shape[0] // total * rows
    memory = pl.BlockSpec(memory_space=pltpu.VMEM)
    return pl.pallas_call(
        update_kernel,
        out_shape=jax.ShapeDtypeStruct(flat.shape, jnp.float32),
        grid_spec=pltpu.PrefetchScalarGridSpec(
            num_scalar_prefetch=1,
            grid=(total // rows,),
            in_specs=[
                pl.BlockSpec((lines, LANES), lambda i, order: (i, 0)),
                pl.BlockSpec((rows, depth), lambda i, order: (i, 0)),
                memory,
            ],
            out_specs=pl.BlockSpec((lines, LANES), lambda i, order: (i, 0)),
            scratch_shapes=[pltpu.VMEM((rows, 3 * depth), jnp.bfloat16)],
        ),
        compiler_params=pltpu.CompilerParams(vmem_limit_bytes=56 << 20),
    )(order, flat, left, parts)


def local(covariance, panel_order):
    row_count, slots, _, width = covariance.shape
    owners = lax.axis_size("blk")
    planes = lax.axis_size("rows")
    depth = SECTIONS * width
    row_panels = row_count // width
    panels, blocks = gather(panel_order, covariance)

    if owners == 8 and row_panels == 2 * owners and planes > 1 and SECTIONS == 2 and width % (8 * CHUNKS) == 0:
        left, parts = exchange(panel_order, panels, blocks, planes, width)
        left = left.reshape(row_count, depth)
    else:
        targets = [panel_order[section] for section in range(SECTIONS)]
        strips = [
            lax.dynamic_slice_in_dim(covariance, (target % row_panels) * width, width, 0).reshape(width, slots * width)
            for target in targets
        ]
        own = jnp.concatenate(strips, axis=0)
        roots = jnp.stack([target // row_panels for target in targets])
        here = jnp.repeat(roots == lax.axis_index("rows"), width)
        right = lax.psum(jnp.where(here[:, None], own, 0.0), "rows").T
        left = lax.psum(panels, "blk")
        parts = solve(panel_order, lax.psum(blocks, ("blk", "rows")), right)

    flat = covariance.reshape(row_count * slots * (width // LANES), LANES)
    return update(panel_order, flat, left, parts).reshape(covariance.shape)


def solution(mesh):
    return jax.shard_map(
        local,
        mesh=mesh,
        in_specs=(P("rows", None, "blk", None), P()),
        out_specs=P("rows", None, "blk", None),
        check_vma=False,
    )
```

```python
import functools

import jax
import jax.numpy as jnp
from jax import lax
from jax.experimental import pallas as pl
from jax.experimental.pallas import tpu as pltpu
from jax.sharding import PartitionSpec as P

SECTIONS = 2
LANES = 128
CHUNKS = 8
HOP = 1
AHEAD = 2
TILE = 128
SUB = 8
RANK = 8
FACTOR_AT = 6
ROWS = 256
MESH = pl.DeviceIdType.MESH
HIGHEST = lax.Precision.HIGHEST


def split(values):
    high = values.astype(jnp.bfloat16)
    low = (values - high.astype(jnp.float32)).astype(jnp.bfloat16)
    return high, low


def gather_kernel(order_ref, covariance_ref, panels_ref, blocks_ref, sems):
    me = lax.axis_index("blk")
    z = lax.axis_index("rows")
    owners = lax.axis_size("blk")
    row_count, _, _, width = covariance_ref.shape
    row_panels = row_count // width
    targets = [order_ref[section] for section in range(SECTIONS)]
    mine = [lax.rem(target, owners) == me for target in targets]

    def fetch(section, i):
        rows = pl.ds(i * width, width)
        return pltpu.make_async_copy(
            covariance_ref.at[rows, lax.div(targets[section], owners), 0, :],
            panels_ref.at[rows, pl.ds(section * width, width)],
            sems.at[section, i],
        )

    for section in range(SECTIONS):
        @pl.when(mine[section])
        def _():
            for i in range(row_panels):
                fetch(section, i).start()

        @pl.when(jnp.logical_not(mine[section]))
        def _():
            panels_ref[:, section * width : (section + 1) * width] = jnp.zeros((row_count, width), jnp.float32)

    for section in range(SECTIONS):
        @pl.when(mine[section])
        def _():
            for i in range(row_panels):
                fetch(section, i).wait()

    at = 0
    for r in range(SECTIONS):
        for c in range(r + 1):
            root = lax.div(targets[r], row_panels)
            rows = pl.ds(pl.multiple_of(lax.rem(targets[r], row_panels) * width, width), width)
            seen = panels_ref[rows, c * width : (c + 1) * width]
            blocks_ref[at : at + width, :] = jnp.where(root == z, seen, 0.0)
            at += width


def gather(order, covariance):
    row_count, _, _, width = covariance.shape
    count = SECTIONS * (SECTIONS + 1) // 2
    memory = pl.BlockSpec(memory_space=pltpu.VMEM)
    return pl.pallas_call(
        gather_kernel,
        out_shape=(
            jax.ShapeDtypeStruct((row_count, SECTIONS * width), jnp.float32),
            jax.ShapeDtypeStruct((count * width, width), jnp.float32),
        ),
        grid_spec=pltpu.PrefetchScalarGridSpec(
            num_scalar_prefetch=1,
            grid=(),
            in_specs=[pl.BlockSpec(memory_space=pl.ANY)],
            out_specs=(memory, memory),
            scratch_shapes=[pltpu.SemaphoreType.DMA((SECTIONS, row_count // width))],
        ),
        compiler_params=pltpu.CompilerParams(vmem_limit_bytes=24 << 20),
    )(order, covariance)


def product(a, b, dims):
    return lax.dot_general(a, b, (dims, ((), ())), precision=HIGHEST, preferred_element_type=jnp.float32)


def eliminate(left, right, scales, start, count):
    size = left[0].shape[1]
    index = lax.broadcasted_iota(jnp.int32, (SUB, size), 0)
    for k in range(start, start + count, RANK):
        at, inner = divmod(k, SUB)
        entry = [
            [jnp.broadcast_to(left[at][inner + p : inner + p + 1, k + j : k + j + 1], (1, size)) for j in range(RANK)]
            for p in range(RANK)
        ]
        columns = [
            [jnp.broadcast_to(left[i][:, k + j : k + j + 1], (SUB, size)) for j in range(RANK)]
            for i in range(at, len(left))
        ]
        inverse, ratio = [], [[None] * RANK for _ in range(RANK)]
        for p in range(RANK):
            inverse.append(1.0 / entry[p][p])
            scales[at] = jnp.where(index == inner + p, lax.rsqrt(entry[p][p]), scales[at])
            for j in range(p + 1, RANK):
                ratio[j][p] = entry[p][j] * inverse[p]
            for j in range(p + 1, RANK):
                for m in range(j, RANK):
                    entry[j][m] = entry[j][m] - ratio[j][p] * entry[p][m]
        rows = []
        for j in range(RANK):
            l = left[at][inner + j : inner + j + 1, :]
            r = right[at][inner + j : inner + j + 1, :]
            for p in range(j):
                l = l - ratio[j][p] * rows[p][0]
                r = r - ratio[j][p] * rows[p][1]
            rows.append((l, r))
        rows = [(l * inverse[j], r * inverse[j]) for j, (l, r) in enumerate(rows)]
        for i in range(at, len(left)):
            column = columns[i - at]
            for j in range(RANK):
                for p in range(j):
                    column[j] = column[j] - ratio[j][p] * column[p]
            for j in range(RANK):
                c = jnp.where(index > inner + j, column[j], 0.0) if i == at else column[j]
                left[i] = left[i] - c * rows[j][0]
                right[i] = right[i] - c * rows[j][1]


def invert_tile(tile):
    size = tile.shape[0]
    row_of = lax.broadcasted_iota(jnp.int32, (size, size), 0)
    column_of = lax.broadcasted_iota(jnp.int32, (size, size), 1)
    unit = jnp.where(row_of == column_of, 1.0, 0.0).astype(jnp.float32)
    left = [tile[i : i + SUB] for i in range(0, size, SUB)]
    right = [unit[i : i + SUB] for i in range(0, size, SUB)]
    scales = [jnp.zeros((SUB, size), jnp.float32) for _ in left]
    eliminate(left, right, scales, 0, size)
    return jnp.concatenate([r * s for r, s in zip(right, scales)], axis=0)


def factor_tile(i, work, lower, tiles):
    at = pl.ds(pl.multiple_of(i * TILE, TILE), TILE)
    tile = invert_tile(work[at, at])
    tiles[i] = tile
    below = product(work[:, at], tile, ((1,), (1,)))
    row_of = lax.broadcasted_iota(jnp.int32, below.shape, 0)
    below = jnp.where(row_of >= (i + 1) * TILE, below, 0.0)
    lower[:, at] = below
    work[...] -= product(below, below, ((1,), (1,)))


def factor_start(blocks, work):
    width = blocks.shape[1]
    work[...] = jnp.zeros_like(work)
    block = 0
    for r in range(SECTIONS):
        for c in range(r + 1):
            work[r * width : (r + 1) * width, c * width : (c + 1) * width] = blocks[block : block + width, :]
            block += width


def factor_end(lower, tiles, inverse_ref, whole_ref):
    inverse_ref[...] = jnp.zeros_like(inverse_ref)
    for i in range(tiles.shape[0]):
        at = slice(i * TILE, (i + 1) * TILE)
        inverse_ref[at, at] = tiles[i]
        if i:
            done = slice(0, i * TILE)
            seen = product(lower[at, done], inverse_ref[done, done], ((1,), (0,)))
            inverse_ref[at, done] = -product(tiles[i], seen, ((1,), (0,)))
    inverse = inverse_ref[...]
    whole_ref[...] = product(inverse, inverse, ((0,), (0,)))


def factor_scratch(size):
    return [
        pltpu.VMEM((size, size), jnp.float32),
        pltpu.VMEM((size, size), jnp.float32),
        pltpu.VMEM((size // TILE, TILE, TILE), jnp.float32),
        pltpu.VMEM((size, size), jnp.float32),
        pltpu.VMEM((size, size), jnp.float32),
    ]


def prepare(order_ref, slot, cells, inverse_ref, whole_ref, parts_ref):
    width, depth = cells.shape
    me = lax.axis_index("blk")
    owners = lax.axis_size("blk")
    value = product(whole_ref[...], cells, ((1,), (1,)))
    for section in range(SECTIONS):
        solved = -inverse_ref[section * width : (section + 1) * width, :].T
        value = jnp.where(order_ref[section] == slot * owners + me, solved, value)
    high, low = split(value)
    parts_ref[slot, :depth, :] = high
    parts_ref[slot, depth : 2 * depth, :] = low
    parts_ref[slot, 2 * depth :, :] = high


def solve_kernel(order_ref, blocks_ref, cells_ref, parts_ref, work, lower, tiles, inverse, whole):
    width = blocks_ref.shape[1]
    factor_start(blocks_ref[...], work)

    def one(i, carry):
        factor_tile(i, work, lower, tiles)
        return carry

    lax.fori_loop(0, tiles.shape[0], one, 0)
    factor_end(lower, tiles, inverse, whole)
    for slot in range(parts_ref.shape[0]):
        prepare(order_ref, slot, cells_ref[slot * width : (slot + 1) * width, :], inverse, whole, parts_ref)


def solve(order, blocks, cells):
    width = blocks.shape[1]
    depth = SECTIONS * width
    memory = pl.BlockSpec(memory_space=pltpu.VMEM)
    return pl.pallas_call(
        solve_kernel,
        out_shape=jax.ShapeDtypeStruct((cells.shape[0] // width, 3 * depth, width), jnp.bfloat16),
        in_specs=[pl.BlockSpec(memory_space=pltpu.SMEM), memory, memory],
        out_specs=memory,
        scratch_shapes=factor_scratch(depth),
        compiler_params=pltpu.CompilerParams(vmem_limit_bytes=48 << 20),
    )(order, blocks, cells)


def exchange_kernel(
    planes, order_ref, x_ref, d_ref, left_ref, parts_ref, mine, right_ref, block_ref, mix, one, two,
    d_pair, d_one, d_two, d_plane, e_pair, e_one, e_two, diagonal, work, lower, tiles, inverse, whole,
    s_pair, r_pair, s_one, r_one, s_two, r_two, s_near, r_near, s_far, r_far, s_mate, r_mate,
    s_up, r_up, s_down, r_down, s_block, r_block, s_plane, r_plane, s_mine, s_own,
):
    z = lax.axis_index("rows")
    me = lax.axis_index("blk")
    last = planes - 1
    chip, core = me // 2, me % 2
    y, x = chip // 2, chip % 2
    across = (y * 2 + 1 - x) * 2 + core
    along = ((1 - y) * 2 + x) * 2 + core
    pair = chip * 2 + 1 - core
    rows = mine.shape[3] // CHUNKS

    def lines(c):
        if c is None:
            return slice(None)
        return pl.ds(pl.multiple_of(c * rows, 8), rows)

    def send(src, dst, send_sem, recv_sem, who):
        return pltpu.make_async_remote_copy(
            src_ref=src, dst_ref=dst, send_sem=send_sem, recv_sem=recv_sem,
            device_id=who, device_id_type=MESH,
        )

    def to_pair(c):
        return send(x_ref.at[:, :, :, 1 - core, lines(c)], mix.at[:, :, :, lines(c)],
                    s_pair.at[0], r_pair.at[0 if c is None else c], {"blk": pair})

    def bring(c):
        return pltpu.make_async_copy(x_ref.at[:, :, :, core, lines(c)], mine.at[:, :, :, lines(c)], s_mine.at[c])

    def keep(c):
        here = left_ref.at[:, y, x, core, lines(c)]
        return pltpu.make_async_copy(right_ref.at[z, :, lines(c)], here, s_own.at[c])

    def first(h, c):
        src = mix.at[0, :, 1 - x, lines(c)] if h == 0 else mix.at[1, 1 - y, :, lines(c)]
        return send(src, one.at[h, :, lines(c)], s_one.at[h], r_one.at[h, 0 if c is None else c], {"blk": along if h else across})

    def second(h, c):
        src = one.at[0, 1 - y, lines(c)] if h == 0 else one.at[1, 1 - x, lines(c)]
        return send(src, two.at[h, lines(c)], s_two.at[h], r_two.at[h, 0 if c is None else c], {"blk": across if h else along})

    def near(h, c):
        here = left_ref.at[:, y, x, core, lines(c)]
        return send(right_ref.at[z, :, lines(c)], here, s_near.at[h], r_near.at[h, 0 if c is None else c], {"blk": along if h else across})

    def far(h, c):
        here = left_ref.at[0, y, 1 - x, core, lines(c)] if h == 0 else left_ref.at[1, 1 - y, x, core, lines(c)]
        return send(here, here, s_far.at[h], r_far.at[h, 0 if c is None else c], {"blk": across if h else along})

    def to_mate(c):
        here = left_ref.at[:, :, :, core, lines(c)]
        return send(here, here, s_mate.at[0], r_mate.at[0], {"blk": pair})

    def up(o, c, step=1):
        here = right_ref.at[o, :, lines(c)]
        return send(here, here, s_up.at[o], r_up.at[o, 0 if c is None else c], {"rows": z + step})

    def down(o, c, step=1):
        here = right_ref.at[o, :, lines(c)]
        return send(here, here, s_down.at[o], r_down.at[o, 0 if c is None else c], {"rows": z - step})

    def block_step(j):
        if j == 0:
            return send(d_ref.at[1 - core], d_pair, s_block.at[0], r_block.at[0], {"blk": pair})
        if j == 1:
            return send(e_pair.at[1 - x], d_one, s_block.at[1], r_block.at[1], {"blk": across})
        if j == 2:
            return send(e_one.at[1 - y], d_two, s_block.at[2], r_block.at[2], {"blk": along})
        here = [block_ref.at[core, x, y], block_ref.at[core, x], block_ref.at[core]][j - 4]
        return send(here, here, s_block.at[j - 1], r_block.at[j - 1], {"blk": [along, across, pair][j - 4]})

    def block_plane(i):
        other = lax.rem(z + i, planes)
        return send(e_two, d_plane.at[i - 1], s_plane.at[i - 1], r_plane.at[i - 1], {"rows": other})

    barrier = pltpu.get_barrier_semaphore()
    for who in (across, along, pair):
        pl.semaphore_signal(barrier, inc=1, device_id={"blk": who}, device_id_type=MESH)
    for i in range(1, planes):
        pl.semaphore_signal(barrier, inc=1, device_id={"rows": lax.rem(z + i, planes)}, device_id_type=MESH)
    pl.semaphore_wait(barrier, 3 + last)

    block_step(0).start()

    def begin(c, carry):
        to_pair(c).start()
        bring(c).start()
        return carry

    lax.fori_loop(0, AHEAD, begin, 0)

    def when(c, *conditions):
        valid = jnp.logical_and(c >= 0, c < CHUNKS)
        for condition in conditions:
            valid = jnp.logical_and(valid, condition)
        return pl.when(valid)

    def blocks(j):
        if j == 0:
            block_step(0).wait_recv()
            e_pair[...] = d_ref[core] + d_pair[...]
            block_step(1).start()
        elif j == 1:
            block_step(1).wait_recv()
            e_one[...] = e_pair[x] + d_one[...]
            block_step(2).start()
        elif j == 2:
            block_step(2).wait_recv()
            e_two[...] = e_one[y] + d_two[...]
            for i in range(1, planes):
                block_plane(i).start()
        elif j == 3:
            total = e_two[...]
            for i in range(1, planes):
                block_plane(i).wait_recv()
                total = total + d_plane[i - 1]
            block_ref[core, x, y] = total
            block_step(4).start()
        else:
            block_step(j).wait_recv()
            if j < 6:
                block_step(j + 1).start()

    def block_stages(t):
        for j in range(7):
            @pl.when(t == j)
            def _():
                blocks(j)

    def factor_stages(t):
        count = tiles.shape[0]
        piece = block_ref.shape[3]

        @pl.when(t == FACTOR_AT)
        def _():
            for k in range(8):
                diagonal[k * piece : (k + 1) * piece, :] = block_ref[k // 4, k // 2 % 2, k % 2]
            factor_start(diagonal[...], work)

        @pl.when(jnp.logical_and(t >= FACTOR_AT, t < FACTOR_AT + count))
        def _():
            factor_tile(t - FACTOR_AT, work, lower, tiles)

        @pl.when(t == FACTOR_AT + count)
        def _():
            factor_end(lower, tiles, inverse, whole)

    def solve_cells(o):
        for h in range(2):
            prepare(order_ref, 2 * o + h, right_ref[o, h], inverse, whole, parts_ref)

    def step(t, carry):
        block_stages(t)
        c = t

        @when(c)
        def _():
            to_pair(c).wait_recv()
            bring(c).wait()

            @pl.when(c + AHEAD < CHUNKS)
            def _():
                to_pair(c + AHEAD).start()
                bring(c + AHEAD).start()

            mix[:, :, :, lines(c)] = mix[:, :, :, lines(c)] + mine[:, :, :, lines(c)]
            first(0, c).start()
            first(1, c).start()

        c1 = t - 1

        @when(c1)
        def _():
            first(0, c1).wait_recv()
            one[0, :, lines(c1)] = one[0, :, lines(c1)] + mix[0, :, x, lines(c1)]
            second(0, c1).start()
            first(1, c1).wait_recv()
            one[1, :, lines(c1)] = one[1, :, lines(c1)] + mix[1, y, :, lines(c1)]
            second(1, c1).start()

        c2 = t - 2

        @when(c2)
        def _():
            second(0, c2).wait_recv()
            a = one[0, y, lines(c2)] + two[0, lines(c2)]
            right_ref[z, 0, lines(c2)] = a
            second(1, c2).wait_recv()
            b = one[1, x, lines(c2)] + two[1, lines(c2)]
            right_ref[z, 1, lines(c2)] = b

            @pl.when(z < last)
            def _():
                up(z, c2).start()

            @pl.when(z > 0)
            def _():
                down(z, c2).start()

            keep(c2).start()
            near(0, c2).start()
            near(1, c2).start()

        for distance in range(1, planes):
            e = t - 2 - HOP * distance

            @when(e, z - distance >= 0)
            def _():
                up(z - distance, e, 0).wait_recv()

                @pl.when(z < last)
                def _():
                    up(z - distance, e).start()

            @when(e, z + distance <= last)
            def _():
                down(z + distance, e, 0).wait_recv()

                @pl.when(z > 0)
                def _():
                    down(z + distance, e).start()

        c3 = t - 4

        @when(c3)
        def _():
            near(0, c3).wait_recv()
            far(0, c3).start()
            near(1, c3).wait_recv()
            far(1, c3).start()

        c4 = t - 6

        @when(c4)
        def _():
            far(0, c4).wait_recv()
            far(1, c4).wait_recv()
            keep(c4).wait()
            to_mate(c4).start()

        factor_stages(t)

        for distance in range(planes):
            now = t == CHUNKS + max(FACTOR_AT + 5 - CHUNKS, 1 + HOP * distance)

            @pl.when(jnp.logical_and(now, z - distance >= 0))
            def _():
                solve_cells(z - distance)

            if distance:
                @pl.when(jnp.logical_and(now, z + distance <= last))
                def _():
                    solve_cells(z + distance)

        return carry

    lax.fori_loop(0, CHUNKS + max(6, 2 + HOP * last), step, 0)
    to_mate(None).wait_recv()
    for j in (0, 1, 2, 4, 5, 6):
        block_step(j).wait_send()
    for i in range(1, planes):
        block_plane(i).wait_send()
    to_pair(None).wait_send()
    to_mate(None).wait_send()
    for h in range(2):
        first(h, None).wait_send()
        second(h, None).wait_send()
        near(h, None).wait_send()
        far(h, None).wait_send()
    for distance in range(planes - 1):
        @pl.when(jnp.logical_and(z - distance >= 0, z < last))
        def _():
            up(z - distance, None).wait_send()

        @pl.when(jnp.logical_and(z + distance <= last, z > 0))
        def _():
            down(z + distance, None).wait_send()


def exchange(order, panels, blocks, planes, width):
    depth = panels.shape[1]
    piece = blocks.shape[0] // 8
    dma = pltpu.SemaphoreType.DMA
    memory = pl.BlockSpec(memory_space=pltpu.VMEM)

    def flow(*shape):
        return pltpu.VMEM(shape, jnp.float32)

    return pl.pallas_call(
        functools.partial(exchange_kernel, planes),
        out_shape=(
            jax.ShapeDtypeStruct((2, 2, 2, 2, width, depth), jnp.float32),
            jax.ShapeDtypeStruct((2 * planes, 3 * depth, width), jnp.bfloat16),
        ),
        in_specs=[pl.BlockSpec(memory_space=pltpu.SMEM), pl.BlockSpec(memory_space=pl.ANY), memory],
        out_specs=(pl.BlockSpec(memory_space=pl.ANY), memory),
        scratch_shapes=[
            flow(2, 2, 2, width, depth), flow(planes, 2, width, depth), flow(2, 2, 2, piece, width),
            flow(2, 2, 2, width, depth), flow(2, 2, width, depth), flow(2, width, depth),
            flow(2, 2, piece, width), flow(2, piece, width), flow(piece, width), flow(planes - 1, piece, width),
            flow(2, 2, piece, width), flow(2, piece, width), flow(piece, width), flow(8 * piece, width),
        ] + factor_scratch(depth)
        + [dma((1,)), dma((CHUNKS,))] + [dma((2,)), dma((2, CHUNKS))] * 4 + [dma((1,))] * 2
        + [dma((planes,)), dma((planes, CHUNKS))] * 2 + [dma((6,))] * 2 + [dma((planes - 1,))] * 2 + [dma((CHUNKS,))] * 2,
        compiler_params=pltpu.CompilerParams(
            collective_id=0, has_side_effects=True, vmem_limit_bytes=40 << 20
        ),
    )(order, panels.reshape(2, 2, 2, 2, width, depth), blocks.reshape(2, 2, 2, piece, width))


def update_kernel(order_ref, old_ref, left_ref, parts_ref, out_ref, left_parts):
    slots, _, width = parts_ref.shape
    rows, depth = left_ref.shape
    lines = old_ref.shape[0] // rows
    halves = width // LANES
    me = lax.axis_index("blk")
    owners = lax.axis_size("blk")

    def matches(section, slot):
        return order_ref[section] == slot * owners + me

    high, low = split(left_ref[...])
    left_parts[:, :depth] = high
    left_parts[:, depth : 2 * depth] = high
    left_parts[:, 2 * depth :] = low
    for slot in range(slots):
        change = jnp.dot(left_parts[...], parts_ref[slot], preferred_element_type=jnp.float32)
        gone = matches(0, slot)
        for section in range(1, SECTIONS):
            gone = jnp.logical_or(gone, matches(section, slot))
        for half in range(halves):
            at = pl.ds(slot * halves + half, rows, stride=lines)
            out_ref[at, :] = jnp.where(gone, 0.0, old_ref[at, :]) - change[:, half * LANES : (half + 1) * LANES]


def update(order, flat, left, parts):
    total, depth = left.shape
    rows = min(ROWS, total)
    lines = flat.shape[0] // total * rows
    memory = pl.BlockSpec(memory_space=pltpu.VMEM)
    return pl.pallas_call(
        update_kernel,
        out_shape=jax.ShapeDtypeStruct(flat.shape, jnp.float32),
        grid_spec=pltpu.PrefetchScalarGridSpec(
            num_scalar_prefetch=1,
            grid=(total // rows,),
            in_specs=[
                pl.BlockSpec((lines, LANES), lambda i, order: (i, 0)),
                pl.BlockSpec((rows, depth), lambda i, order: (i, 0)),
                memory,
            ],
            out_specs=pl.BlockSpec((lines, LANES), lambda i, order: (i, 0)),
            scratch_shapes=[pltpu.VMEM((rows, 3 * depth), jnp.bfloat16)],
        ),
        compiler_params=pltpu.CompilerParams(vmem_limit_bytes=56 << 20),
    )(order, flat, left, parts)


def local(covariance, panel_order):
    row_count, slots, _, width = covariance.shape
    owners = lax.axis_size("blk")
    planes = lax.axis_size("rows")
    depth = SECTIONS * width
    row_panels = row_count // width
    panels, blocks = gather(panel_order, covariance)

    if owners == 8 and row_panels == 2 * owners and planes > 1 and SECTIONS == 2 and width % (8 * CHUNKS) == 0:
        left, parts = exchange(panel_order, panels, blocks, planes, width)
        left = left.reshape(row_count, depth)
    else:
        targets = [panel_order[section] for section in range(SECTIONS)]
        strips = [
            lax.dynamic_slice_in_dim(covariance, (target % row_panels) * width, width, 0).reshape(width, slots * width)
            for target in targets
        ]
        own = jnp.concatenate(strips, axis=0)
        roots = jnp.stack([target // row_panels for target in targets])
        here = jnp.repeat(roots == lax.axis_index("rows"), width)
        right = lax.psum(jnp.where(here[:, None], own, 0.0), "rows").T
        left = lax.psum(panels, "blk")
        parts = solve(panel_order, lax.psum(blocks, ("blk", "rows")), right)

    flat = covariance.reshape(row_count * slots * (width // LANES), LANES)
    return update(panel_order, flat, left, parts).reshape(covariance.shape)


def solution(mesh):
    return jax.shard_map(
        local,
        mesh=mesh,
        in_specs=(P("rows", None, "blk", None), P()),
        out_specs=P("rows", None, "blk", None),
        check_vma=False,
    )
```
